1024 devices in a mesh: slow: 32 (over y, x_hi, core), fast: 32 (over x_lo, z).
Axes of the slice: x: 4 (x_hi: 2, x_lo: 2; x = x_hi * 2 + x_lo), y: 8, z: 16, core: 2. Of those that a mesh axis runs over, the one named last changes fastest.
Arguments:
- query_act: bfloat16 [131072, 512], P(('slow', 'fast')), may hold values from -6 to 6
- key_act: bfloat16 [131072, 512], P(('slow', 'fast')), may hold values from -6 to 6
- value_act: bfloat16 [131072, 512], P(('slow', 'fast')), may hold values from -6 to 6
- long_filter: bfloat16 [131072, 32], P(('slow', 'fast')), may hold values from -4 to 4
- out_grad: bfloat16 [131072, 512], P(('slow', 'fast')), may hold values from -6 to 6
Outputs:
- mixed_out: bfloat16 [131072, 512], P(('slow', 'fast'))
- query_grad: bfloat16 [131072, 512], P(('slow', 'fast'))
- key_grad: bfloat16 [131072, 512], P(('slow', 'fast'))
- value_grad: bfloat16 [131072, 512], P(('slow', 'fast'))
- filter_grad: float32 [131072, 32], P(('slow', 'fast'))
The draws below stay inside these ranges and needn't reach their ends.
All inputs are finite; a program needn't handle non-finite values.
Results may differ from the reference program's by a relative error of at most 0.0049.
Values may be sent and summed in bfloat16 or wider, within the bound.
A program may use at most 32 MiB of HBM per device.

```python
import math
import jax
import jax.numpy as jnp
from jax import lax

SLAB = 512
GROUP_CH = 16
FILTER_GROUPS = 32
SEQUENCE_TOKENS = 131072


def draw_long_filter(key, part):
    random_keys = jax.random.split(key, 7)
    delay_index = jnp.arange(SEQUENCE_TOKENS, dtype=jnp.int32)[:, None]
    choose_slow = jax.random.uniform(random_keys[0], (FILTER_GROUPS,))
    is_slow = choose_slow < 0.5
    slow_rate = jnp.exp(jax.random.uniform(random_keys[1], (FILTER_GROUPS,), minval=math.log(0.3 / SEQUENCE_TOKENS), maxval=math.log(2.3 / SEQUENCE_TOKENS)))
    fast_rate = jax.random.uniform(random_keys[2], (FILTER_GROUPS,), minval=1.0 / 50.0, maxval=1.0 / 30.0)
    decay_rate = jnp.where(is_slow, slow_rate, fast_rate)
    spike_delays = jax.random.randint(random_keys[3], (3, FILTER_GROUPS), 1, SEQUENCE_TOKENS)
    spike_retained = jax.random.uniform(random_keys[4], (3, FILTER_GROUPS), minval=0.5, maxval=0.8)
    decay_profile = jnp.exp(-decay_rate[None, :] * delay_index.astype(jnp.float32))
    for spike_index in range(3):
        decay_profile = decay_profile * jnp.where(delay_index >= spike_delays[spike_index][None, :], spike_retained[spike_index][None, :], 1.0)
    factor_spread = jnp.exp(jax.random.uniform(random_keys[5], (SEQUENCE_TOKENS, FILTER_GROUPS), minval=-0.7, maxval=0.7))
    rough_part = jax.random.normal(random_keys[6], (SEQUENCE_TOKENS, FILTER_GROUPS))
    energy = -jnp.expm1(-2.0 * decay_rate) / -jnp.expm1(-2.0 * decay_rate * SEQUENCE_TOKENS)
    taps = rough_part * factor_spread * decay_profile * jnp.sqrt(energy / 1.36)[None, :]
    return taps.astype(jnp.bfloat16)


def steps_of(key, shape, shards, smallest, top_value):
    gain = 1.0
    for axis_at, blocks in shards:
        steps = jax.random.uniform(jax.random.fold_in(jax.random.fold_in(key, 6), axis_at), (blocks,), jnp.float32, smallest / len(shards), top_value / len(shards))
        gain = gain * jnp.repeat(jnp.exp(steps), shape[axis_at] // blocks).reshape((-1,) + (1,) * (len(shape) - 1 - axis_at))
    return gain


def bell_draw(stream_key, shape, scale, reach, shards=(), kind=jnp.bfloat16):
    entries = scale * jax.random.normal(stream_key, shape, jnp.float32)
    if shards:
        entries = entries * steps_of(stream_key, shape, shards, -0.22, 0.18)
    return jnp.clip(entries, -reach, reach).astype(kind)


def setup_inputs(seed: int = 0) -> dict:
    seeds = jax.random.split(jax.random.key(seed), 6)
    query_act = bell_draw(seeds[0], (SEQUENCE_TOKENS, SLAB), 1.0, 6.0, ((0, 1024),))
    key_act = bell_draw(seeds[1], (SEQUENCE_TOKENS, SLAB), 1.0, 6.0, ((0, 1024),))
    value_act = bell_draw(seeds[2], (SEQUENCE_TOKENS, SLAB), 1.0, 6.0, ((0, 1024),))
    long_filter = draw_long_filter(jax.random.fold_in(seeds[5], 71), 0)
    out_grad = bell_draw(seeds[4], (SEQUENCE_TOKENS, SLAB), 1.0, 6.0, ((0, 1024),))
    return {"query_act": query_act, "key_act": key_act, "value_act": value_act, "long_filter": long_filter, "out_grad": out_grad}


def group_terms(product, grad_in, filter_taps):
    points = 2 * SEQUENCE_TOKENS
    taps_spec = jnp.fft.rfft(filter_taps, points)
    prod_spec = jnp.fft.rfft(product, points, axis=0)
    grad_spec = jnp.fft.rfft(grad_in, points, axis=0)
    convolved = jnp.fft.irfft(prod_spec * taps_spec[:, None], points, axis=0)[:SEQUENCE_TOKENS]
    backward = jnp.fft.irfft(grad_spec * jnp.conj(taps_spec)[:, None], points, axis=0)[:SEQUENCE_TOKENS]
    correlation = jnp.fft.irfft(lax.optimization_barrier(jnp.sum(grad_spec * jnp.conj(prod_spec), axis=1)), points)[:SEQUENCE_TOKENS]
    return (convolved, backward, correlation)

def reference(query_act, key_act, value_act, long_filter, out_grad):
    scale = 1.0 / math.sqrt(SEQUENCE_TOKENS * GROUP_CH)

    def per_group(buffers, group_id):
        first_col = group_id * GROUP_CH

        def columns(values):
            return lax.dynamic_slice_in_dim(values, first_col, GROUP_CH, axis=1).astype(jnp.float32)
        query_cols = columns(query_act)
        key_cols = columns(key_act)
        value_cols = columns(value_act)
        grad_cols = columns(out_grad)
        product = lax.optimization_barrier((key_cols * value_cols).astype(jnp.bfloat16)).astype(jnp.float32)
        grad_in = lax.optimization_barrier((grad_cols * query_cols).astype(jnp.bfloat16)).astype(jnp.float32)
        filter_taps = lax.dynamic_slice_in_dim(long_filter, group_id, 1, axis=1)[:, 0].astype(jnp.float32)
        convolved, backward, correlation = group_terms(product, grad_in, filter_taps)
        results = (query_cols * convolved, grad_cols * convolved, backward * value_cols, backward * key_cols)
        updated = tuple((lax.dynamic_update_slice_in_dim(buffer_old, result_new.astype(jnp.bfloat16), first_col, axis=1) for buffer_old, result_new in zip(buffers, results)))
        return (updated, correlation * scale)
    empty = jnp.zeros((SEQUENCE_TOKENS, SLAB), jnp.bfloat16)
    buffers, correlations = lax.scan(per_group, (empty, empty, empty, empty), jnp.arange(FILTER_GROUPS, dtype=jnp.int32))
    return (buffers[0], buffers[1], buffers[2], buffers[3], jnp.transpose(correlations))
```

```python
import functools
import math

import jax
import jax.numpy as jnp
from jax import lax
from jax.experimental import pallas as pl
from jax.experimental.pallas import tpu as pltpu
from jax.sharding import PartitionSpec as P

MESH = pl.DeviceIdType.MESH
f32 = jnp.float32
bf16 = jnp.bfloat16
LANES = 128
BLOCK = 4


def times_const(value, factor):
    re, im = value
    a, b = factor.real, factor.imag
    if abs(b) < 1e-12:
        if abs(a - 1.0) < 1e-12:
            return re, im
        return re * a, im * a
    if abs(a) < 1e-12:
        return (-im, re) if b > 0 else (im, -re)
    return re * a - im * b, re * b + im * a


def unit(turns):
    return complex(math.cos(2.0 * math.pi * turns), math.sin(2.0 * math.pi * turns))


def dft(values, sign):
    count = len(values)
    if count == 1:
        return values
    even, odd = dft(values[0::2], sign), dft(values[1::2], sign)
    first, second = [], []
    for k in range(count // 2):
        turned = times_const(odd[k], unit(sign * k / count))
        first.append((even[k][0] + turned[0], even[k][1] + turned[1]))
        second.append((even[k][0] - turned[0], even[k][1] - turned[1]))
    return first + second


def lead_forward(values):
    count = len(values)
    twisted = []
    for f, value in enumerate(values):
        w = unit(-f / (4.0 * count))
        twisted.append((value * w.real, value * w.imag))
    return dft(twisted, -1.0)


def lead_inverse(values, scale):
    count = len(values)
    result = []
    for f, (re, im) in enumerate(dft(values, 1.0)):
        w = unit(f / (4.0 * count)) * scale
        result.append(re * w.real - im * w.imag)
    return result


def all_sent(buf, sem, count):
    view = buf.at[pl.ds(0, count - 1)]
    pltpu.make_async_copy(view, view, sem).wait()


def kernel(
    slow_count, fast_count, corr_scale,
    q_ref, k_ref, v_ref, h_ref, o_ref,
    mixed_ref, qgrad_ref, kgrad_ref, vgrad_ref, fgrad_ref,
    send_f, got_f, send_fh, got_fh,
    send_s, got_s, send_sh, got_sh,
    spec, taps, trow, drow, dbuf, mixes,
    send_b, got_b, send_bh, got_bh,
    send_c, got_c, send_ch,
    basis_hi, basis_lo, basis_f32, inv_hi, inv_lo, inv_f32,
    ssem, rsem,
):
    slow = lax.axis_index("slow")
    fast = lax.axis_index("fast")
    S, F = slow_count, fast_count

    barrier = pltpu.get_barrier_semaphore()

    def greet_fast(o, carry):
        pl.semaphore_signal(
            barrier, inc=1, device_id=(slow, lax.rem(fast + o, F)), device_id_type=MESH
        )
        return carry

    def greet_slow(o, carry):
        pl.semaphore_signal(
            barrier, inc=1, device_id=(lax.rem(slow + o, S), fast), device_id_type=MESH
        )
        return carry

    lax.fori_loop(1, F, greet_fast, 0)
    lax.fori_loop(1, S, greet_slow, 0)

    def push(axis, src, dst, which):
        count = F if axis == "fast" else S
        me = fast if axis == "fast" else slow

        def one(o, carry):
            to = lax.rem(me + o, count)
            device = (slow, to) if axis == "fast" else (to, fast)
            pltpu.make_async_remote_copy(
                src_ref=src.at[to],
                dst_ref=dst.at[me],
                send_sem=ssem.at[which],
                recv_sem=rsem.at[which],
                device_id=device,
                device_id_type=MESH,
            ).start()
            return carry

        lax.fori_loop(1, count, one, 0)
        dst[me] = src[me]

    product = (k_ref[...].astype(f32) * v_ref[...].astype(f32)).T
    send_f[:, 0:16, :] = product.reshape(F, 16, LANES).astype(bf16)
    grad_in = (o_ref[...].astype(f32) * q_ref[...].astype(f32)).T
    send_f[:, 16:32, :] = grad_in.reshape(F, 16, LANES).astype(bf16)
    send_fh[...] = h_ref[...]
    pl.semaphore_wait(barrier, F + S - 2)
    push("fast", send_fh, got_fh, 0)
    push("fast", send_f, got_f, 1)

    b = lax.broadcasted_iota(jnp.int32, (LANES, LANES), 0)
    k2 = lax.broadcasted_iota(jnp.int32, (LANES, LANES), 1)
    period = 4 * LANES * F
    phase = jnp.bitwise_and((4 * slow + 1) * b + 4 * F * (k2 * b), period - 1)
    angle = phase.astype(f32) * (2.0 * math.pi / period)
    wr, wi = jnp.cos(angle), -jnp.sin(angle)
    basis_f32[0:LANES, 0:LANES] = wr
    basis_f32[0:LANES, LANES:] = wi
    basis_f32[LANES:, 0:LANES] = -wi
    basis_f32[LANES:, LANES:] = wr
    wrt, wit = wr.T, wi.T
    inv_f32[0:LANES, 0:LANES] = wrt
    inv_f32[0:LANES, LANES:] = -wit
    inv_f32[LANES:, 0:LANES] = wit
    inv_f32[LANES:, LANES:] = wrt
    for full, hi, lo in ((basis_f32, basis_hi, basis_lo), (inv_f32, inv_hi, inv_lo)):
        top = full[...].astype(bf16)
        hi[...] = top
        lo[...] = (full[...] - top.astype(f32)).astype(bf16)

    for at in range(BLOCK - 1):
        spec[at] = jnp.zeros((32, 2 * LANES), f32)
        taps[at] = jnp.zeros((8, 2 * LANES), f32)

    all_sent(got_fh, rsem.at[0], F)
    for k, (re, im) in enumerate(lead_forward([got_fh[f] for f in range(F)])):
        send_sh[k, :, 0:LANES] = re
        send_sh[k, :, LANES:] = im
    push("slow", send_sh, got_sh, 2)
    all_sent(got_f, rsem.at[1], F)

    def lead(g, carry):
        rows = pl.ds(pl.multiple_of(g * 16, 16), 16)
        out = lead_forward([got_f[f, rows, :].astype(f32) for f in range(F)])
        for k, (re, im) in enumerate(out):
            send_s[k, rows, 0:LANES] = re.astype(bf16)
            send_s[k, rows, LANES:] = im.astype(bf16)
        return carry

    lax.fori_loop(0, 2, lead, 0)
    push("slow", send_s, got_s, 3)

    all_sent(got_sh, rsem.at[2], S)
    for i in range(S):
        trow[i : i + 1, :] = got_sh[i]
    tap_spec = jnp.dot(
        trow[0:S, :], basis_f32[...], precision=lax.Precision.HIGHEST, preferred_element_type=f32
    )
    trow[0:8, :] = jnp.zeros((8, 2 * LANES), f32)
    trow[8 : 8 + S, :] = tap_spec
    before = trow[7 : 7 + S, :]
    tap_re = tap_spec[:, 0:LANES] - before[:, LANES:]
    tap_im = tap_spec[:, LANES:] + before[:, 0:LANES]
    for d in range(S):
        taps[BLOCK - 1 + d, :, 0:LANES] = jnp.broadcast_to(tap_re[d : d + 1], (8, LANES))
        taps[BLOCK - 1 + d, :, LANES:] = jnp.broadcast_to(tap_im[d : d + 1], (8, LANES))

    all_sent(got_s, rsem.at[3], S)
    step = min(8, S)

    def to_spec(n, carry):
        at = pl.multiple_of(n * step, step)
        x = got_s[pl.ds(at, step)].reshape(step * 32, 2 * LANES)
        y = jnp.dot(x, basis_hi[...], preferred_element_type=f32)
        y += jnp.dot(x, basis_lo[...], preferred_element_type=f32)
        spec[pl.ds(at + BLOCK - 1, step)] = y.reshape(step, 32, 2 * LANES)
        return carry

    lax.fori_loop(0, S // step, to_spec, 0)

    def part(at, row, im):
        lo = LANES if im else 0
        return spec[at, row : row + 8, lo : lo + LANES]

    zero = jnp.zeros((8, LANES), f32)
    off = BLOCK - 1

    def convolve(J, carry):
        def inner(i, acc):
            rows = [(part(off + i, r, False), part(off + i, r, True)) for r in (0, 8)]
            result = []
            for jj in range(BLOCK):
                d = off + BLOCK * J + jj - i
                hr, hi = taps[d, :, 0:LANES], taps[d, :, LANES:]
                for n, (pr, pi) in enumerate(rows):
                    re, im = acc[2 * jj + n]
                    result.append((re + (hr * pr - hi * pi), im + (hr * pi + hi * pr)))
            return tuple(result)

        acc = lax.fori_loop(0, BLOCK * (J + 1), inner, ((zero, zero),) * (2 * BLOCK))
        for jj in range(BLOCK):
            for n in range(2):
                re, im = acc[2 * jj + n]
                mixes[BLOCK * J + jj, 8 * n : 8 * n + 8, 0:LANES] = re
                mixes[BLOCK * J + jj, 8 * n : 8 * n + 8, LANES:] = im
        return carry

    def correlate(J, carry):
        def inner(i, accs):
            acc, cor = accs
            rows = [(part(off + i, r, False), part(off + i, r, True)) for r in (16, 24)]
            result, sums = [], []
            for jj in range(BLOCK):
                d = off + i - BLOCK * J - jj
                hr, hi = taps[d, :, 0:LANES], taps[d, :, LANES:]
                cr, ci = cor[jj]
                for n, (gr, gi) in enumerate(rows):
                    re, im = acc[2 * jj + n]
                    result.append((re + (hr * gr + hi * gi), im + (hr * gi - hi * gr)))
                    pr, pi = part(d, 8 * n, False), part(d, 8 * n, True)
                    cr = cr + (gr * pr + gi * pi)
                    ci = ci + (gi * pr - gr * pi)
                sums.append((cr, ci))
            return tuple(result), tuple(sums)

        acc, cor = lax.fori_loop(
            BLOCK * J, S, inner, (((zero, zero),) * (2 * BLOCK), ((zero, zero),) * BLOCK)
        )
        for jj in range(BLOCK):
            for n in range(2):
                re, im = acc[2 * jj + n]
                mixes[BLOCK * J + jj, 16 + 8 * n : 24 + 8 * n, 0:LANES] = re
                mixes[BLOCK * J + jj, 16 + 8 * n : 24 + 8 * n, LANES:] = im
            cr, ci = cor[jj]
            dbuf[BLOCK * J + jj, :, 0:LANES] = jnp.sum(cr, axis=0, keepdims=True)
            dbuf[BLOCK * J + jj, :, LANES:] = jnp.sum(ci, axis=0, keepdims=True)
        return carry

    lax.fori_loop(0, S // BLOCK, convolve, 0)
    lax.fori_loop(0, S // BLOCK, correlate, 0)

    def from_spec(n, carry):
        at = pl.ds(pl.multiple_of(n * step, step), step)
        z = mixes[at].reshape(step * 32, 2 * LANES)
        hi = z.astype(bf16)
        lo = (z - hi.astype(f32)).astype(bf16)
        y = jnp.dot(hi, inv_hi[...], preferred_element_type=f32)
        y += jnp.dot(hi, inv_lo[...], preferred_element_type=f32)
        y += jnp.dot(lo, inv_hi[...], preferred_element_type=f32)
        send_b[at] = y.reshape(step, 32, 2 * LANES).astype(bf16)
        return carry

    lax.fori_loop(0, S // step, from_spec, 0)
    push("slow", send_b, got_b, 4)

    drow[...] = jnp.zeros(drow.shape, f32)
    for j in range(S):
        drow[j : j + 1, :] = dbuf[j]
    here, after = drow[0:S, :], drow[1 : S + 1, :]
    corr = jnp.concatenate(
        (here[:, 0:LANES] + after[:, LANES:], here[:, LANES:] - after[:, 0:LANES]), axis=1
    )
    corr = jnp.dot(
        corr, inv_f32[...], precision=lax.Precision.HIGHEST, preferred_element_type=f32
    )
    for j in range(S):
        send_bh[j] = corr[j : j + 1, :]
    push("slow", send_bh, got_bh, 5)

    scale = 1.0 / (LANES * F)
    all_sent(got_b, rsem.at[4], S)

    def unlead(g, carry):
        rows = pl.ds(pl.multiple_of(g * 16, 16), 16)
        values = [
            (got_b[k, rows, 0:LANES].astype(f32), got_b[k, rows, LANES:].astype(f32))
            for k in range(F)
        ]
        for f, out in enumerate(lead_inverse(values, scale)):
            send_c[f, rows, :] = out.astype(bf16)
        return carry

    lax.fori_loop(0, 2, unlead, 0)
    push("fast", send_c, got_c, 6)
    all_sent(got_bh, rsem.at[5], S)
    values = [(got_bh[k, :, 0:LANES], got_bh[k, :, LANES:]) for k in range(F)]
    for f, out in enumerate(lead_inverse(values, scale * corr_scale)):
        send_ch[f] = out
    push("fast", send_ch, fgrad_ref, 7)

    all_sent(got_c, rsem.at[6], F)
    convolved = got_c[:, 0:16, :].astype(f32).reshape(F * 16, LANES).T
    mixed_ref[...] = (q_ref[...].astype(f32) * convolved).astype(bf16)
    qgrad_ref[...] = (o_ref[...].astype(f32) * convolved).astype(bf16)
    backward = got_c[:, 16:32, :].astype(f32).reshape(F * 16, LANES).T
    kgrad_ref[...] = (backward * v_ref[...].astype(f32)).astype(bf16)
    vgrad_ref[...] = (backward * k_ref[...].astype(f32)).astype(bf16)
    all_sent(fgrad_ref, rsem.at[7], F)

    for which, buf, count in (
        (0, send_fh, F), (1, send_f, F), (2, send_sh, S), (3, send_s, S),
        (4, send_b, S), (5, send_bh, S), (6, send_c, F), (7, send_ch, F),
    ):
        all_sent(buf, ssem.at[which], count)


def on_device(slow_count, fast_count, query_act, key_act, value_act, long_filter, out_grad):
    tokens, channels = query_act.shape
    groups = long_filter.shape[1]
    S, F = slow_count, fast_count
    width = channels // groups
    seq_length = tokens * S * F
    corr_scale = 1.0 / math.sqrt(seq_length * width)
    rows = 2 * width
    taps_rows = jnp.transpose(long_filter.astype(f32)).reshape(groups, 1, tokens)
    wide = jax.ShapeDtypeStruct((tokens, channels), bf16)
    vmem = pl.BlockSpec(memory_space=pltpu.VMEM)

    def chunks(count, height, lanes, kind):
        return pltpu.VMEM((count, height, lanes), kind)

    L, L2 = LANES, 2 * LANES
    outs = pl.pallas_call(
        functools.partial(kernel, S, F, corr_scale),
        out_shape=(wide, wide, wide, wide, jax.ShapeDtypeStruct((groups, 1, tokens), f32)),
        in_specs=[vmem] * 5,
        out_specs=(vmem,) * 5,
        scratch_shapes=[
            chunks(F, rows, L, bf16), chunks(F, rows, L, bf16),
            chunks(F, 1, L, f32), chunks(F, 1, L, f32),
            chunks(S, rows, L2, bf16), chunks(S, rows, L2, bf16),
            chunks(S, 1, L2, f32), chunks(S, 1, L2, f32),
            chunks(S + BLOCK - 1, rows, L2, f32),
            chunks(S + BLOCK - 1, 8, L2, f32),
            pltpu.VMEM((S + 8, L2), f32),
            pltpu.VMEM((S + 8, L2), f32),
            chunks(S, 1, L2, f32),
            chunks(S, rows, L2, f32),
            chunks(S, rows, L2, bf16), chunks(S, rows, L2, bf16),
            chunks(S, 1, L2, f32), chunks(S, 1, L2, f32),
            chunks(F, rows, L, bf16), chunks(F, rows, L, bf16),
            chunks(F, 1, L, f32),
            pltpu.VMEM((L2, L2), bf16), pltpu.VMEM((L2, L2), bf16), pltpu.VMEM((L2, L2), f32),
            pltpu.VMEM((L2, L2), bf16), pltpu.VMEM((L2, L2), bf16), pltpu.VMEM((L2, L2), f32),
            pltpu.SemaphoreType.DMA((8,)),
            pltpu.SemaphoreType.DMA((8,)),
        ],
        compiler_params=pltpu.CompilerParams(
            collective_id=0, has_side_effects=True, vmem_limit_bytes=40 << 20
        ),
    )(query_act, key_act, value_act, taps_rows, out_grad)
    filter_grad = jnp.transpose(outs[4].reshape(groups, tokens))
    return outs[0], outs[1], outs[2], outs[3], filter_grad


def solution(mesh):
    placed = P(("slow", "fast"), None)
    return jax.shard_map(
        functools.partial(on_device, mesh.shape["slow"], mesh.shape["fast"]),
        mesh=mesh,
        in_specs=(placed,) * 5,
        out_specs=(placed,) * 5,
        check_vma=False,
    )
```

```python
import functools
import math

import jax
import jax.numpy as jnp
from jax import lax
from jax.experimental import pallas as pl
from jax.experimental.pallas import tpu as pltpu
from jax.sharding import PartitionSpec as P

MESH = pl.DeviceIdType.MESH
f32 = jnp.float32
bf16 = jnp.bfloat16
LANES = 128
PARTS = 4
ROWS = 8


def times_const(value, factor):
    re, im = value
    a, b = factor.real, factor.imag
    if abs(b) < 1e-12:
        if abs(a - 1.0) < 1e-12:
            return re, im
        return re * a, im * a
    if abs(a) < 1e-12:
        return (-im, re) if b > 0 else (im, -re)
    return re * a - im * b, re * b + im * a


def unit(turns):
    return complex(math.cos(2.0 * math.pi * turns), math.sin(2.0 * math.pi * turns))


def dft(values, sign):
    count = len(values)
    if count == 1:
        return values
    even, odd = dft(values[0::2], sign), dft(values[1::2], sign)
    first, second = [], []
    for k in range(count // 2):
        turned = times_const(odd[k], unit(sign * k / count))
        first.append((even[k][0] + turned[0], even[k][1] + turned[1]))
        second.append((even[k][0] - turned[0], even[k][1] - turned[1]))
    return first + second


def lead_forward(values):
    count = len(values)
    twisted = []
    for f, value in enumerate(values):
        w = unit(-f / (4.0 * count))
        twisted.append((value * w.real, value * w.imag))
    return dft(twisted, -1.0)


def lead_inverse(values, scale):
    count = len(values)
    result = []
    for f, (re, im) in enumerate(dft(values, 1.0)):
        w = unit(f / (4.0 * count)) * scale
        result.append(re * w.real - im * w.imag)
    return result


def arrived(buf, sem, count):
    view = buf.at[pl.ds(0, count - 1)]
    pltpu.make_async_copy(view, view, sem).wait()


def for_peers(me, ring, side, visit):
    fast_major = side == 2
    at = lax.rem(me, ring) if fast_major else lax.div(me, side)
    beside = lax.div(me, ring) if fast_major else lax.rem(me, side)

    def at_distance(d, skip):
        there = lax.rem(at + d, ring)
        for a in range(skip, side):
            other = lax.rem(beside + a, side)
            visit(other * ring + there if fast_major else there * side + other)

    half = ring // 2
    if half:
        at_distance(half, 0)

    def pair(i, carry):
        at_distance(half - i, 0)
        at_distance(half + i, 0)
        return carry

    if half > 1:
        lax.fori_loop(1, half, pair, 0)
    at_distance(0, 1)


def exchange_kernel(
    S, F, corr_scale,
    q_hbm, k_hbm, v_hbm, h_hbm, o_hbm,
    mixed_out_hbm, corr_hbm,
    q_ref, k_ref, v_ref, h_ref, o_ref,
    send_f, got_f, send_fh, got_fh,
    send_s, got_s, send_sh, got_sh,
    spec, taps, trow, drow, dbuf, mixes,
    send_b, got_b, send_bh, got_bh,
    send_c, send_ch,
    basis_hi, basis_lo, basis_f32, inv_hi, inv_lo, inv_f32,
    ssem, rsem, lsem,
):
    slow = lax.axis_index("slow")
    fast = lax.axis_index("fast")
    block = min(8, S)
    off = block - 1

    loads = [
        pltpu.make_async_copy(src, dst, lsem.at[n])
        for n, (src, dst) in enumerate(
            ((k_hbm, k_ref), (v_hbm, v_ref), (h_hbm, h_ref), (o_hbm, o_ref), (q_hbm, q_ref))
        )
    ]
    barrier = pltpu.get_barrier_semaphore()

    def greet_fast(to):
        pl.semaphore_signal(barrier, inc=1, device_id=(slow, to), device_id_type=MESH)

    def greet_slow(to):
        pl.semaphore_signal(barrier, inc=1, device_id=(to, fast), device_id_type=MESH)

    for_peers(fast, F // 2, 2, greet_fast)
    for_peers(slow, S // 4, 4, greet_slow)
    for load in loads:
        load.start()

    def push(axis, src, dst, which):
        def one(to):
            pltpu.make_async_remote_copy(
                src_ref=src.at[to],
                dst_ref=dst.at[fast if axis == "fast" else slow],
                send_sem=ssem.at[which],
                recv_sem=rsem.at[which],
                device_id=(slow, to) if axis == "fast" else (to, fast),
                device_id_type=MESH,
            ).start()

        if axis == "fast":
            for_peers(fast, F // 2, 2, one)
        else:
            for_peers(slow, S // 4, 4, one)

    for load in loads[:3]:
        load.wait()
    for g, row in enumerate(jnp.split(h_ref[...].astype(f32), F)):
        send_fh[g] = row
    product = (k_ref[...].astype(f32) * v_ref[...].astype(f32)).T.reshape(F, 16, LANES)
    send_f[0] = product[:, 0:8].astype(bf16)
    send_f[2] = product[:, 8:16].astype(bf16)
    pl.semaphore_wait(barrier, F + S - 2)
    push("fast", send_fh, got_fh, 4)
    push("fast", send_f.at[0], got_f.at[0], 0)
    for load in loads[3:]:
        load.wait()
    grad_in = (o_ref[...].astype(f32) * q_ref[...].astype(f32)).T.reshape(F, 16, LANES)
    send_f[1] = grad_in[:, 0:8].astype(bf16)
    send_f[3] = grad_in[:, 8:16].astype(bf16)
    for part in range(1, PARTS):
        push("fast", send_f.at[part], got_f.at[part], part)
    got_fh[fast] = send_fh[fast]
    for part in range(PARTS):
        got_f[part, fast] = send_f[part, fast]

    b = lax.broadcasted_iota(jnp.int32, (LANES, LANES), 0)
    k2 = lax.broadcasted_iota(jnp.int32, (LANES, LANES), 1)
    period = 4 * LANES * F
    phase = jnp.bitwise_and((4 * slow + 1) * b + 4 * F * (k2 * b), period - 1)
    angle = phase.astype(f32) * (2.0 * math.pi / period)
    wr, wi = jnp.cos(angle), -jnp.sin(angle)
    basis_f32[0:LANES, 0:LANES] = wr
    basis_f32[0:LANES, LANES:] = wi
    basis_f32[LANES:, 0:LANES] = -wi
    basis_f32[LANES:, LANES:] = wr
    wrt, wit = wr.T, wi.T
    inv_f32[0:LANES, 0:LANES] = wrt
    inv_f32[0:LANES, LANES:] = -wit
    inv_f32[LANES:, 0:LANES] = wit
    inv_f32[LANES:, LANES:] = wrt
    for full, hi, lo in ((basis_f32, basis_hi, basis_lo), (inv_f32, inv_hi, inv_lo)):
        top = full[...].astype(bf16)
        hi[...] = top
        lo[...] = (full[...] - top.astype(f32)).astype(bf16)

    for at in range(off):
        spec[0, at] = jnp.zeros((ROWS, 2 * LANES), f32)
        spec[2, at] = jnp.zeros((ROWS, 2 * LANES), f32)
        taps[at] = jnp.zeros((ROWS, 2 * LANES), f32)
    dbuf[...] = jnp.zeros(dbuf.shape, f32)

    arrived(got_fh, rsem.at[4], F)
    for k, (re, im) in enumerate(lead_forward([got_fh[f] for f in range(F)])):
        send_sh[k, :, 0:LANES] = re
        send_sh[k, :, LANES:] = im
    push("slow", send_sh, got_sh, 9)
    got_sh[slow] = send_sh[slow]

    def lead(part, carry):
        arrived(got_f.at[part], rsem.at[part], F)
        out = lead_forward([got_f[part, f].astype(f32) for f in range(F)])
        for k, (re, im) in enumerate(out):
            send_s[part, k, :, 0:LANES] = re.astype(bf16)
            send_s[part, k, :, LANES:] = im.astype(bf16)
        push("slow", send_s.at[part], got_s.at[part], 5 + part)
        got_s[part, slow] = send_s[part, slow]
        return carry

    lax.fori_loop(0, PARTS, lead, 0)

    arrived(got_sh, rsem.at[9], S)
    for i in range(S):
        trow[i : i + 1, :] = got_sh[i]
    tap_spec = jnp.dot(
        trow[0:S, :], basis_f32[...], precision=lax.Precision.HIGHEST, preferred_element_type=f32
    )
    trow[0:8, :] = jnp.zeros((8, 2 * LANES), f32)
    trow[8 : 8 + S, :] = tap_spec
    before = trow[7 : 7 + S, :]
    tap_re = tap_spec[:, 0:LANES] - before[:, LANES:]
    tap_im = tap_spec[:, LANES:] + before[:, 0:LANES]
    for d in range(S):
        taps[off + d, :, 0:LANES] = jnp.broadcast_to(tap_re[d : d + 1], (ROWS, LANES))
        taps[off + d, :, LANES:] = jnp.broadcast_to(tap_im[d : d + 1], (ROWS, LANES))

    step = min(16, S)

    def to_spec(part):
        arrived(got_s.at[part], rsem.at[5 + part], S)

        def some(n, carry):
            at = pl.multiple_of(n * step, step)
            x = got_s[part, pl.ds(at, step)].astype(f32).reshape(step * ROWS, 2 * LANES).astype(bf16)
            y = jnp.dot(x, basis_hi[...], preferred_element_type=f32)
            y += jnp.dot(x, basis_lo[...], preferred_element_type=f32)
            spec[part, pl.ds(at + off, step)] = y.reshape(step, ROWS, 2 * LANES)
            return carry

        lax.fori_loop(0, S // step, some, 0)

    def from_spec(part):
        def some(n, carry):
            at = pl.ds(pl.multiple_of(n * step, step), step)
            z = mixes[at].reshape(step * ROWS, 2 * LANES)
            hi = z.astype(bf16)
            lo = (z - hi.astype(f32)).astype(bf16)
            y = jnp.dot(hi, inv_hi[...], preferred_element_type=f32)
            y += jnp.dot(hi, inv_lo[...], preferred_element_type=f32)
            y += jnp.dot(lo, inv_hi[...], preferred_element_type=f32)
            send_b[part, at] = y.reshape(step, ROWS, 2 * LANES).astype(bf16)
            return carry

        lax.fori_loop(0, S // step, some, 0)
        push("slow", send_b.at[part], got_b.at[part], 10 + part)
        got_b[part, slow] = send_b[part, slow]

    def both(ref, *at):
        return ref[(*at, slice(None), slice(0, LANES))], ref[(*at, slice(None), slice(LANES, None))]

    zero = jnp.zeros((ROWS, LANES), f32)

    def convolve(part):
        def group(J, carry):
            def inner(i, acc):
                pr, pi = both(spec, part, off + i)
                result = []
                for jj in range(block):
                    hr, hi = both(taps, off + block * J + jj - i)
                    re, im = acc[jj]
                    result.append((re + (hr * pr - hi * pi), im + (hr * pi + hi * pr)))
                return tuple(result)

            acc = lax.fori_loop(0, block * (J + 1), inner, ((zero, zero),) * block)
            for jj in range(block):
                mixes[block * J + jj, :, 0:LANES], mixes[block * J + jj, :, LANES:] = acc[jj]
            return carry

        lax.fori_loop(0, S // block, group, 0)

    def correlate(part):
        def group(J, carry):
            def inner(i, accs):
                gr, gi = both(spec, part, off + i)
                result = []
                for jj in range(block):
                    d = off + i - block * J - jj
                    hr, hi = both(taps, d)
                    pr, pi = both(spec, part - 1, d)
                    re, im, cr, ci = accs[jj]
                    result.append((
                        re + (hr * gr + hi * gi), im + (hr * gi - hi * gr),
                        cr + (gr * pr + gi * pi), ci + (gi * pr - gr * pi),
                    ))
                return tuple(result)

            accs = lax.fori_loop(block * J, S, inner, ((zero,) * 4,) * block)
            for jj in range(block):
                re, im, cr, ci = accs[jj]
                mixes[block * J + jj, :, 0:LANES] = re
                mixes[block * J + jj, :, LANES:] = im
                dbuf[block * J + jj, :, 0:LANES] += jnp.sum(cr, axis=0, keepdims=True)
                dbuf[block * J + jj, :, LANES:] += jnp.sum(ci, axis=0, keepdims=True)
            return carry

        lax.fori_loop(0, S // block, group, 0)

    def mix(n, carry):
        to_spec(2 * n)
        convolve(2 * n)
        from_spec(2 * n)
        to_spec(2 * n + 1)
        correlate(2 * n + 1)
        from_spec(2 * n + 1)
        return carry

    lax.fori_loop(0, PARTS // 2, mix, 0)

    drow[...] = jnp.zeros(drow.shape, f32)
    for j in range(S):
        drow[j : j + 1, :] = dbuf[j]
    here, after = drow[0:S, :], drow[1 : S + 1, :]
    corr = jnp.concatenate(
        (here[:, 0:LANES] + after[:, LANES:], here[:, LANES:] - after[:, 0:LANES]), axis=1
    )
    corr = jnp.dot(
        corr, inv_f32[...], precision=lax.Precision.HIGHEST, preferred_element_type=f32
    )
    for j in range(S):
        send_bh[j] = corr[j : j + 1, :]
    push("slow", send_bh, got_bh, 14)
    got_bh[slow] = send_bh[slow]

    scale = 1.0 / (LANES * F)

    def unlead(part, carry):
        arrived(got_b.at[part], rsem.at[10 + part], S)
        values = []
        for k in range(F):
            re, im = both(got_b, part, k)
            values.append((re.astype(f32), im.astype(f32)))
        for f, out in enumerate(lead_inverse(values, scale)):
            send_c[part, f] = out.astype(bf16)
        push("fast", send_c.at[part], mixed_out_hbm.at[part], 15 + part)
        pltpu.make_async_copy(
            send_c.at[part, fast], mixed_out_hbm.at[part, fast], lsem.at[5 + part]
        ).start()
        return carry

    lax.fori_loop(0, PARTS, unlead, 0)
    arrived(got_bh, rsem.at[14], S)
    values = [both(got_bh, k) for k in range(F)]
    for f, out in enumerate(lead_inverse(values, scale * corr_scale)):
        send_ch[f] = out
    push("fast", send_ch, corr_hbm, 19)
    own = pltpu.make_async_copy(send_ch.at[fast], corr_hbm.at[fast], lsem.at[9])
    own.start()

    for part in range(PARTS):
        arrived(send_f.at[part], ssem.at[part], F)
        arrived(send_s.at[part], ssem.at[5 + part], S)
        arrived(send_b.at[part], ssem.at[10 + part], S)
        arrived(send_c.at[part], ssem.at[15 + part], F)
        pltpu.make_async_copy(
            send_c.at[part, fast], mixed_out_hbm.at[part, fast], lsem.at[5 + part]
        ).wait()
        arrived(mixed_out_hbm.at[part], rsem.at[15 + part], F)
    for which, buf, count in ((4, send_fh, F), (9, send_sh, S), (14, send_bh, S), (19, send_ch, F)):
        arrived(buf, ssem.at[which], count)
    own.wait()
    arrived(corr_hbm, rsem.at[19], F)


def gate_kernel(
    c_hbm, corr_hbm, q_hbm, k_hbm, v_hbm, o_hbm,
    mixed_hbm, qgrad_hbm, kgrad_hbm, vgrad_hbm, fgrad_hbm,
    c_ref, corr_ref, q_ref, k_ref, v_ref, o_ref,
    mixed_ref, qgrad_ref, kgrad_ref, vgrad_ref, fgrad_ref, sem,
):
    groups, tokens = corr_ref.shape[0], corr_ref.shape[2]
    loads = [
        pltpu.make_async_copy(src, dst, sem.at[n])
        for n, (src, dst) in enumerate((
            (c_hbm, c_ref), (q_hbm, q_ref), (o_hbm, o_ref),
            (k_hbm, k_ref), (v_hbm, v_ref), (corr_hbm, corr_ref),
        ))
    ]
    for load in loads:
        load.start()

    def channels(part):
        low, high = c_ref[part].astype(f32), c_ref[part + 2].astype(f32)
        return jnp.concatenate((low, high), axis=1).reshape(groups * 16, tokens).T

    stores = []

    def store(src, dst):
        stores.append(pltpu.make_async_copy(src, dst, sem.at[len(loads) + len(stores)]))
        stores[-1].start()

    for load in loads[:3]:
        load.wait()
    convolved = channels(0)
    mixed_ref[...] = (q_ref[...].astype(f32) * convolved).astype(bf16)
    store(mixed_ref, mixed_hbm)
    qgrad_ref[...] = (o_ref[...].astype(f32) * convolved).astype(bf16)
    store(qgrad_ref, qgrad_hbm)
    for load in loads[3:]:
        load.wait()
    backward = channels(1)
    kgrad_ref[...] = (backward * v_ref[...].astype(f32)).astype(bf16)
    store(kgrad_ref, kgrad_hbm)
    vgrad_ref[...] = (backward * k_ref[...].astype(f32)).astype(bf16)
    store(vgrad_ref, vgrad_hbm)
    fgrad_ref[...] = corr_ref[...].reshape(groups, tokens)
    store(fgrad_ref, fgrad_hbm)
    for done in stores:
        done.wait()


def on_device(S, F, query_act, key_act, value_act, long_filter, out_grad):
    tokens, channels = query_act.shape
    groups = long_filter.shape[1]
    seq_length = tokens * S * F
    corr_scale = 1.0 / math.sqrt(seq_length * (channels // groups))
    wide = jax.ShapeDtypeStruct((tokens, channels), bf16)
    hbm = pl.BlockSpec(memory_space=pltpu.HBM)
    L, L2 = LANES, 2 * LANES
    off = min(8, S) - 1
    wides = [pltpu.VMEM(wide.shape, bf16)] * 4
    parts = jax.ShapeDtypeStruct((PARTS, F, ROWS, tokens), bf16)
    corrs = jax.ShapeDtypeStruct((F, 1, tokens), f32)
    mixed, corr = pl.pallas_call(
        functools.partial(exchange_kernel, S, F, corr_scale),
        out_shape=(parts, corrs),
        in_specs=[hbm] * 5,
        out_specs=(hbm,) * 2,
        scratch_shapes=[
            *wides[:3], pltpu.VMEM((groups, tokens), bf16), wides[3],
            pltpu.VMEM((PARTS, F, ROWS, L), bf16), pltpu.VMEM((PARTS, F, ROWS, L), bf16),
            pltpu.VMEM((F, 1, L), f32), pltpu.VMEM((F, 1, L), f32),
            pltpu.VMEM((PARTS, S, ROWS, L2), bf16), pltpu.VMEM((PARTS, S, ROWS, L2), bf16),
            pltpu.VMEM((S, 1, L2), f32), pltpu.VMEM((S, 1, L2), f32),
            pltpu.VMEM((PARTS, S + off, ROWS, L2), f32),
            pltpu.VMEM((S + off, ROWS, L2), f32),
            pltpu.VMEM((S + 8, L2), f32),
            pltpu.VMEM((S + 8, L2), f32),
            pltpu.VMEM((S, 1, L2), f32),
            pltpu.VMEM((S, ROWS, L2), f32),
            pltpu.VMEM((PARTS, S, ROWS, L2), bf16), pltpu.VMEM((PARTS, S, ROWS, L2), bf16),
            pltpu.VMEM((S, 1, L2), f32), pltpu.VMEM((S, 1, L2), f32),
            pltpu.VMEM((PARTS, F, ROWS, L), bf16),
            pltpu.VMEM((F, 1, L), f32),
            pltpu.VMEM((L2, L2), bf16), pltpu.VMEM((L2, L2), bf16), pltpu.VMEM((L2, L2), f32),
            pltpu.VMEM((L2, L2), bf16), pltpu.VMEM((L2, L2), bf16), pltpu.VMEM((L2, L2), f32),
            pltpu.SemaphoreType.DMA((5 * PARTS,)),
            pltpu.SemaphoreType.DMA((5 * PARTS,)),
            pltpu.SemaphoreType.DMA((10,)),
        ],
        compiler_params=pltpu.CompilerParams(
            collective_id=0, has_side_effects=True, vmem_limit_bytes=63 << 20
        ),
    )(query_act, key_act, value_act, long_filter.T, out_grad)
    fgrad = jax.ShapeDtypeStruct((groups, tokens), f32)
    outs = pl.pallas_call(
        gate_kernel,
        out_shape=(wide, wide, wide, wide, fgrad),
        in_specs=[hbm] * 6,
        out_specs=(hbm,) * 5,
        scratch_shapes=[
            pltpu.VMEM(parts.shape, bf16), pltpu.VMEM(corrs.shape, f32),
            *wides, *wides, pltpu.VMEM(fgrad.shape, f32),
            pltpu.SemaphoreType.DMA((11,)),
        ],
        compiler_params=pltpu.CompilerParams(vmem_limit_bytes=63 << 20),
    )(mixed, corr, query_act, key_act, value_act, out_grad)
    return (*outs[:4], outs[4].T)


def solution(mesh):
    placed = P(("slow", "fast"), None)
    return jax.shard_map(
        functools.partial(on_device, mesh.shape["slow"], mesh.shape["fast"]),
        mesh=mesh,
        in_specs=(placed,) * 5,
        out_specs=(placed,) * 5,
        check_vma=False,
    )
```

```python
import functools
import math

import jax
import jax.numpy as jnp
from jax import lax
from jax.experimental import pallas as pl
from jax.experimental.pallas import tpu as pltpu
from jax.sharding import PartitionSpec as P

MESH = pl.DeviceIdType.MESH
f32 = jnp.float32
bf16 = jnp.bfloat16
LANES = 128
PARTS = 4
ROWS = 8


def times_const(value, factor):
    re, im = value
    a, b = factor.real, factor.imag
    if abs(b) < 1e-12:
        if abs(a - 1.0) < 1e-12:
            return re, im
        return re * a, im * a
    if abs(a) < 1e-12:
        return (-im, re) if b > 0 else (im, -re)
    return re * a - im * b, re * b + im * a


def unit(turns):
    return complex(math.cos(2.0 * math.pi * turns), math.sin(2.0 * math.pi * turns))


def dft(values, sign):
    count = len(values)
    if count == 1:
        return values
    even, odd = dft(values[0::2], sign), dft(values[1::2], sign)
    first, second = [], []
    for k in range(count // 2):
        turned = times_const(odd[k], unit(sign * k / count))
        first.append((even[k][0] + turned[0], even[k][1] + turned[1]))
        second.append((even[k][0] - turned[0], even[k][1] - turned[1]))
    return first + second


def lead_forward(values):
    count = len(values)
    twisted = []
    for f, value in enumerate(values):
        w = unit(-f / (4.0 * count))
        twisted.append((value * w.real, value * w.imag))
    return dft(twisted, -1.0)


def lead_inverse(values, scale):
    count = len(values)
    result = []
    for f, (re, im) in enumerate(dft(values, 1.0)):
        w = unit(f / (4.0 * count)) * scale
        result.append(re * w.real - im * w.imag)
    return result


def arrived(buf, sem, count):
    view = buf.at[pl.ds(0, count - 1)]
    pltpu.make_async_copy(view, view, sem).wait()


def for_peers(me, ring, side, visit):
    fast_major = side == 2
    at = lax.rem(me, ring) if fast_major else lax.div(me, side)
    beside = lax.div(me, ring) if fast_major else lax.rem(me, side)

    def at_distance(d, skip):
        there = lax.rem(at + d, ring)
        for a in range(skip, side):
            other = lax.rem(beside + a, side)
            visit(other * ring + there if fast_major else there * side + other)

    half = ring // 2
    if half:
        at_distance(half, 0)

    def pair(i, carry):
        at_distance(half - i, 0)
        at_distance(half + i, 0)
        return carry

    if half > 1:
        lax.fori_loop(1, half, pair, 0)
    at_distance(0, 1)


def exchange_kernel(
    S, F, corr_scale,
    q_hbm, k_hbm, v_hbm, h_hbm, o_hbm,
    mixed_out_hbm, corr_hbm,
    q_ref, k_ref, v_ref, h_ref, o_ref,
    send_f, got_f, send_fh, got_fh,
    send_s, got_s, send_sh, got_sh,
    spec, taps, trow, drow, dbuf, mixes,
    send_b, got_b, send_bh, got_bh,
    send_c, send_ch,
    basis_hi, basis_lo, basis_f32, inv_hi, inv_lo, inv_f32,
    ssem, rsem, lsem,
):
    slow = lax.axis_index("slow")
    fast = lax.axis_index("fast")
    block = min(8, S)
    off = block - 1

    loads = [
        pltpu.make_async_copy(src, dst, lsem.at[n])
        for n, (src, dst) in enumerate(
            ((k_hbm, k_ref), (v_hbm, v_ref), (h_hbm, h_ref), (o_hbm, o_ref), (q_hbm, q_ref))
        )
    ]
    barrier = pltpu.get_barrier_semaphore()

    def greet_fast(to):
        pl.semaphore_signal(barrier, inc=1, device_id=(slow, to), device_id_type=MESH)

    def greet_slow(to):
        pl.semaphore_signal(barrier, inc=1, device_id=(to, fast), device_id_type=MESH)

    for_peers(fast, F // 2, 2, greet_fast)
    for_peers(slow, S // 4, 4, greet_slow)
    for load in loads:
        load.start()

    def push(axis, src, dst, which):
        def one(to):
            pltpu.make_async_remote_copy(
                src_ref=src.at[to],
                dst_ref=dst.at[fast if axis == "fast" else slow],
                send_sem=ssem.at[which],
                recv_sem=rsem.at[which],
                device_id=(slow, to) if axis == "fast" else (to, fast),
                device_id_type=MESH,
            ).start()

        if axis == "fast":
            for_peers(fast, F // 2, 2, one)
        else:
            for_peers(slow, S // 4, 4, one)

    for load in loads[:3]:
        load.wait()
    for g, row in enumerate(jnp.split(h_ref[...].astype(f32), F)):
        send_fh[g] = row
    product = (k_ref[...].astype(f32) * v_ref[...].astype(f32)).T.reshape(F, 16, LANES)
    send_f[0] = product[:, 0:8].astype(bf16)
    send_f[2] = product[:, 8:16].astype(bf16)
    pl.semaphore_wait(barrier, F + S - 2)
    push("fast", send_fh, got_fh, 4)
    push("fast", send_f.at[0], got_f.at[0], 0)
    for load in loads[3:]:
        load.wait()
    grad_in = (o_ref[...].astype(f32) * q_ref[...].astype(f32)).T.reshape(F, 16, LANES)
    send_f[1] = grad_in[:, 0:8].astype(bf16)
    send_f[3] = grad_in[:, 8:16].astype(bf16)
    for part in range(1, PARTS):
        push("fast", send_f.at[part], got_f.at[part], part)
    got_fh[fast] = send_fh[fast]
    for part in range(PARTS):
        got_f[part, fast] = send_f[part, fast]

    b = lax.broadcasted_iota(jnp.int32, (LANES, LANES), 0)
    k2 = lax.broadcasted_iota(jnp.int32, (LANES, LANES), 1)
    period = 4 * LANES * F
    phase = jnp.bitwise_and((4 * slow + 1) * b + 4 * F * (k2 * b), period - 1)
    angle = phase.astype(f32) * (2.0 * math.pi / period)
    wr, wi = jnp.cos(angle), -jnp.sin(angle)
    basis_f32[0:LANES, 0:LANES] = wr
    basis_f32[0:LANES, LANES:] = wi
    basis_f32[LANES:, 0:LANES] = -wi
    basis_f32[LANES:, LANES:] = wr
    wrt, wit = wr.T, wi.T
    inv_f32[0:LANES, 0:LANES] = wrt
    inv_f32[0:LANES, LANES:] = -wit
    inv_f32[LANES:, 0:LANES] = wit
    inv_f32[LANES:, LANES:] = wrt
    for full, hi, lo in ((basis_f32, basis_hi, basis_lo), (inv_f32, inv_hi, inv_lo)):
        top = full[...].astype(bf16)
        hi[...] = top
        lo[...] = (full[...] - top.astype(f32)).astype(bf16)

    for at in range(off):
        spec[0, at] = jnp.zeros((ROWS, 2 * LANES), f32)
        spec[2, at] = jnp.zeros((ROWS, 2 * LANES), f32)
        taps[at] = jnp.zeros((ROWS, 2 * LANES), f32)
    dbuf[...] = jnp.zeros(dbuf.shape, f32)

    arrived(got_fh, rsem.at[4], F)
    for k, (re, im) in enumerate(lead_forward([got_fh[f] for f in range(F)])):
        send_sh[k, :, 0:LANES] = re
        send_sh[k, :, LANES:] = im
    push("slow", send_sh, got_sh, 9)
    got_sh[slow] = send_sh[slow]

    def lead(part, carry):
        arrived(got_f.at[part], rsem.at[part], F)
        out = lead_forward([got_f[part, f].astype(f32) for f in range(F)])
        for k, (re, im) in enumerate(out):
            send_s[part, k, :, 0:LANES] = re.astype(bf16)
            send_s[part, k, :, LANES:] = im.astype(bf16)
        push("slow", send_s.at[part], got_s.at[part], 5 + part)
        got_s[part, slow] = send_s[part, slow]
        return carry

    lax.fori_loop(0, PARTS - 1, lead, 0)

    arrived(got_sh, rsem.at[9], S)
    for i in range(S):
        trow[i : i + 1, :] = got_sh[i]
    tap_spec = jnp.dot(
        trow[0:S, :], basis_f32[...], precision=lax.Precision.HIGHEST, preferred_element_type=f32
    )
    trow[0:8, :] = jnp.zeros((8, 2 * LANES), f32)
    trow[8 : 8 + S, :] = tap_spec
    before = trow[7 : 7 + S, :]
    tap_re = tap_spec[:, 0:LANES] - before[:, LANES:]
    tap_im = tap_spec[:, LANES:] + before[:, 0:LANES]
    for d in range(S):
        taps[off + d, :, 0:LANES] = jnp.broadcast_to(tap_re[d : d + 1], (ROWS, LANES))
        taps[off + d, :, LANES:] = jnp.broadcast_to(tap_im[d : d + 1], (ROWS, LANES))

    lead(PARTS - 1, 0)

    step = min(16, S)

    def to_spec(part):
        arrived(got_s.at[part], rsem.at[5 + part], S)

        def some(n, carry):
            at = pl.multiple_of(n * step, step)
            x = got_s[part, pl.ds(at, step)].astype(f32).reshape(step * ROWS, 2 * LANES).astype(bf16)
            y = jnp.dot(x, basis_hi[...], preferred_element_type=f32)
            y += jnp.dot(x, basis_lo[...], preferred_element_type=f32)
            spec[part, pl.ds(at + off, step)] = y.reshape(step, ROWS, 2 * LANES)
            return carry

        lax.fori_loop(0, S // step, some, 0)

    def from_spec(part):
        def some(n, carry):
            at = pl.ds(pl.multiple_of(n * step, step), step)
            z = mixes[at].reshape(step * ROWS, 2 * LANES)
            hi = z.astype(bf16)
            lo = (z - hi.astype(f32)).astype(bf16)
            y = jnp.dot(hi, inv_hi[...], preferred_element_type=f32)
            y += jnp.dot(hi, inv_lo[...], preferred_element_type=f32)
            y += jnp.dot(lo, inv_hi[...], preferred_element_type=f32)
            send_b[part, at] = y.reshape(step, ROWS, 2 * LANES).astype(bf16)
            return carry

        lax.fori_loop(0, S // step, some, 0)
        push("slow", send_b.at[part], got_b.at[part], 10 + part)
        got_b[part, slow] = send_b[part, slow]

    def both(ref, *at):
        return ref[(*at, slice(None), slice(0, LANES))], ref[(*at, slice(None), slice(LANES, None))]

    zero = jnp.zeros((ROWS, LANES), f32)

    def convolve(part):
        def group(J, carry):
            def inner(i, acc):
                pr, pi = both(spec, part, off + i)
                result = []
                for jj in range(block):
                    hr, hi = both(taps, off + block * J + jj - i)
                    re, im = acc[jj]
                    result.append((re + (hr * pr - hi * pi), im + (hr * pi + hi * pr)))
                return tuple(result)

            acc = lax.fori_loop(0, block * (J + 1), inner, ((zero, zero),) * block)
            for jj in range(block):
                mixes[block * J + jj, :, 0:LANES], mixes[block * J + jj, :, LANES:] = acc[jj]
            return carry

        lax.fori_loop(0, S // block, group, 0)

    def adjoint(part):
        def group(J, carry):
            def inner(i, acc):
                gr, gi = both(spec, part, off + i)
                result = []
                for jj in range(block):
                    hr, hi = both(taps, off + i - block * J - jj)
                    re, im = acc[jj]
                    result.append((re + (hr * gr + hi * gi), im + (hr * gi - hi * gr)))
                return tuple(result)

            acc = lax.fori_loop(block * J, S, inner, ((zero, zero),) * block)
            for jj in range(block):
                mixes[block * J + jj, :, 0:LANES], mixes[block * J + jj, :, LANES:] = acc[jj]
            return carry

        lax.fori_loop(0, S // block, group, 0)

    def correlate(part):
        def group(J, carry):
            def inner(i, acc):
                gr, gi = both(spec, part, off + i)
                result = []
                for jj in range(block):
                    pr, pi = both(spec, part - 1, off + i - block * J - jj)
                    re, im = acc[jj]
                    result.append((re + (gr * pr + gi * pi), im + (gi * pr - gr * pi)))
                return tuple(result)

            acc = lax.fori_loop(block * J, S, inner, ((zero, zero),) * block)
            for jj in range(block):
                re, im = acc[jj]
                dbuf[block * J + jj, :, 0:LANES] += jnp.sum(re, axis=0, keepdims=True)
                dbuf[block * J + jj, :, LANES:] += jnp.sum(im, axis=0, keepdims=True)
            return carry

        lax.fori_loop(0, S // block, group, 0)

    scale = 1.0 / (LANES * F)

    def unlead(part, carry):
        arrived(got_b.at[part], rsem.at[10 + part], S)
        values = []
        for k in range(F):
            re, im = both(got_b, part, k)
            values.append((re.astype(f32), im.astype(f32)))
        for f, out in enumerate(lead_inverse(values, scale)):
            send_c[part, f] = out.astype(bf16)
        push("fast", send_c.at[part], mixed_out_hbm.at[part], 15 + part)
        pltpu.make_async_copy(
            send_c.at[part, fast], mixed_out_hbm.at[part, fast], lsem.at[5 + part]
        ).start()
        return carry

    for part in range(PARTS):
        to_spec(part)
        if part % 2:
            adjoint(part)
        else:
            convolve(part)
        from_spec(part)
        if part == 1:
            correlate(part)
    unlead(0, 0)
    correlate(PARTS - 1)

    drow[...] = jnp.zeros(drow.shape, f32)
    for j in range(S):
        drow[j : j + 1, :] = dbuf[j]
    here, after = drow[0:S, :], drow[1 : S + 1, :]
    corr = jnp.concatenate(
        (here[:, 0:LANES] + after[:, LANES:], here[:, LANES:] - after[:, 0:LANES]), axis=1
    )
    corr = jnp.dot(
        corr, inv_f32[...], precision=lax.Precision.HIGHEST, preferred_element_type=f32
    )
    for j in range(S):
        send_bh[j] = corr[j : j + 1, :]
    push("slow", send_bh, got_bh, 14)
    got_bh[slow] = send_bh[slow]

    lax.fori_loop(1, PARTS, unlead, 0)
    arrived(got_bh, rsem.at[14], S)
    values = [both(got_bh, k) for k in range(F)]
    for f, out in enumerate(lead_inverse(values, scale * corr_scale)):
        send_ch[f] = out
    push("fast", send_ch, corr_hbm, 19)
    own = pltpu.make_async_copy(send_ch.at[fast], corr_hbm.at[fast], lsem.at[9])
    own.start()

    for part in range(PARTS):
        arrived(send_f.at[part], ssem.at[part], F)
        arrived(send_s.at[part], ssem.at[5 + part], S)
        arrived(send_b.at[part], ssem.at[10 + part], S)
        arrived(send_c.at[part], ssem.at[15 + part], F)
        pltpu.make_async_copy(
            send_c.at[part, fast], mixed_out_hbm.at[part, fast], lsem.at[5 + part]
        ).wait()
        arrived(mixed_out_hbm.at[part], rsem.at[15 + part], F)
    for which, buf, count in ((4, send_fh, F), (9, send_sh, S), (14, send_bh, S), (19, send_ch, F)):
        arrived(buf, ssem.at[which], count)
    own.wait()
    arrived(corr_hbm, rsem.at[19], F)


def gate_kernel(
    c_hbm, corr_hbm, q_hbm, k_hbm, v_hbm, o_hbm,
    mixed_hbm, qgrad_hbm, kgrad_hbm, vgrad_hbm, fgrad_hbm,
    c_ref, corr_ref, q_ref, k_ref, v_ref, o_ref,
    mixed_ref, qgrad_ref, kgrad_ref, vgrad_ref, fgrad_ref, sem,
):
    groups, tokens = corr_ref.shape[0], corr_ref.shape[2]
    loads = [
        pltpu.make_async_copy(src, dst, sem.at[n])
        for n, (src, dst) in enumerate((
            (c_hbm, c_ref), (q_hbm, q_ref), (o_hbm, o_ref),
            (k_hbm, k_ref), (v_hbm, v_ref), (corr_hbm, corr_ref),
        ))
    ]
    for load in loads:
        load.start()

    def channels(part):
        low, high = c_ref[part].astype(f32), c_ref[part + 2].astype(f32)
        return jnp.concatenate((low, high), axis=1).reshape(groups * 16, tokens).T

    stores = []

    def store(src, dst):
        stores.append(pltpu.make_async_copy(src, dst, sem.at[len(loads) + len(stores)]))
        stores[-1].start()

    for load in loads[:3]:
        load.wait()
    convolved = channels(0)
    mixed_ref[...] = (q_ref[...].astype(f32) * convolved).astype(bf16)
    store(mixed_ref, mixed_hbm)
    qgrad_ref[...] = (o_ref[...].astype(f32) * convolved).astype(bf16)
    store(qgrad_ref, qgrad_hbm)
    for load in loads[3:]:
        load.wait()
    backward = channels(1)
    kgrad_ref[...] = (backward * v_ref[...].astype(f32)).astype(bf16)
    store(kgrad_ref, kgrad_hbm)
    vgrad_ref[...] = (backward * k_ref[...].astype(f32)).astype(bf16)
    store(vgrad_ref, vgrad_hbm)
    fgrad_ref[...] = corr_ref[...].reshape(groups, tokens)
    store(fgrad_ref, fgrad_hbm)
    for done in stores:
        done.wait()


def on_device(S, F, query_act, key_act, value_act, long_filter, out_grad):
    tokens, channels = query_act.shape
    groups = long_filter.shape[1]
    seq_length = tokens * S * F
    corr_scale = 1.0 / math.sqrt(seq_length * (channels // groups))
    wide = jax.ShapeDtypeStruct((tokens, channels), bf16)
    hbm = pl.BlockSpec(memory_space=pltpu.HBM)
    L, L2 = LANES, 2 * LANES
    off = min(8, S) - 1
    wides = [pltpu.VMEM(wide.shape, bf16)] * 4
    parts = jax.ShapeDtypeStruct((PARTS, F, ROWS, tokens), bf16)
    corrs = jax.ShapeDtypeStruct((F, 1, tokens), f32)
    mixed, corr = pl.pallas_call(
        functools.partial(exchange_kernel, S, F, corr_scale),
        out_shape=(parts, corrs),
        in_specs=[hbm] * 5,
        out_specs=(hbm,) * 2,
        scratch_shapes=[
            *wides[:3], pltpu.VMEM((groups, tokens), bf16), wides[3],
            pltpu.VMEM((PARTS, F, ROWS, L), bf16), pltpu.VMEM((PARTS, F, ROWS, L), bf16),
            pltpu.VMEM((F, 1, L), f32), pltpu.VMEM((F, 1, L), f32),
            pltpu.VMEM((PARTS, S, ROWS, L2), bf16), pltpu.VMEM((PARTS, S, ROWS, L2), bf16),
            pltpu.VMEM((S, 1, L2), f32), pltpu.VMEM((S, 1, L2), f32),
            pltpu.VMEM((PARTS, S + off, ROWS, L2), f32),
            pltpu.VMEM((S + off, ROWS, L2), f32),
            pltpu.VMEM((S + 8, L2), f32),
            pltpu.VMEM((S + 8, L2), f32),
            pltpu.VMEM((S, 1, L2), f32),
            pltpu.VMEM((S, ROWS, L2), f32),
            pltpu.VMEM((PARTS, S, ROWS, L2), bf16), pltpu.VMEM((PARTS, S, ROWS, L2), bf16),
            pltpu.VMEM((S, 1, L2), f32), pltpu.VMEM((S, 1, L2), f32),
            pltpu.VMEM((PARTS, F, ROWS, L), bf16),
            pltpu.VMEM((F, 1, L), f32),
            pltpu.VMEM((L2, L2), bf16), pltpu.VMEM((L2, L2), bf16), pltpu.VMEM((L2, L2), f32),
            pltpu.VMEM((L2, L2), bf16), pltpu.VMEM((L2, L2), bf16), pltpu.VMEM((L2, L2), f32),
            pltpu.SemaphoreType.DMA((5 * PARTS,)),
            pltpu.SemaphoreType.DMA((5 * PARTS,)),
            pltpu.SemaphoreType.DMA((10,)),
        ],
        compiler_params=pltpu.CompilerParams(
            collective_id=0, has_side_effects=True, vmem_limit_bytes=63 << 20
        ),
    )(query_act, key_act, value_act, long_filter.T, out_grad)
    fgrad = jax.ShapeDtypeStruct((groups, tokens), f32)
    outs = pl.pallas_call(
        gate_kernel,
        out_shape=(wide, wide, wide, wide, fgrad),
        in_specs=[hbm] * 6,
        out_specs=(hbm,) * 5,
        scratch_shapes=[
            pltpu.VMEM(parts.shape, bf16), pltpu.VMEM(corrs.shape, f32),
            *wides, *wides, pltpu.VMEM(fgrad.shape, f32),
            pltpu.SemaphoreType.DMA((11,)),
        ],
        compiler_params=pltpu.CompilerParams(vmem_limit_bytes=63 << 20),
    )(mixed, corr, query_act, key_act, value_act, out_grad)
    return (*outs[:4], outs[4].T)


def solution(mesh):
    placed = P(("slow", "fast"), None)
    return jax.shard_map(
        functools.partial(on_device, mesh.shape["slow"], mesh.shape["fast"]),
        mesh=mesh,
        in_specs=(placed,) * 5,
        out_specs=(placed,) * 5,
        check_vma=False,
    )
```
